32 devices in a mesh: gx: 2 (over x), gy: 4 (over y, core), gz: 4 (over z).
Axes of the slice: x: 2, y: 2, z: 4, core: 2. Of those that a mesh axis runs over, the one named last changes fastest.
Arguments:
- right_side: float32 [32, 64, 1024], P('gx', 'gy', 'gz'), may hold values from -5 to 5
- coefficients: float32 [4, 32, 64, 1024], P(None, 'gx', 'gy', 'gz'), may hold values from 0.1 to 32
- first_guess: float32 [32, 64, 1024], P('gx', 'gy', 'gz'), may hold values from -3 to 3
Outputs:
- solution_field: float32 [32, 64, 1024], P('gx', 'gy', 'gz')
The draws below stay inside these ranges and needn't reach their ends.
All inputs are finite; a program needn't handle non-finite values.
Results may differ from the reference program's by a relative error of at most 0.00002.
Values sent between devices are 32-bit elements; how exact they have to be, the bound alone decides.
A program may use at most 128 MiB of HBM per device.

```python
import jax
import jax.numpy as jnp
from jax import lax

CYCLES = 2
SWEEPS = 8
NX = 32
NY = 64
NZ = 1024


slab_width = 64


def draw_coefficients(key, part):
    first_pos = jnp.arange(NX, dtype=jnp.int32)[:, None, None]
    second_pos = jnp.arange(NY, dtype=jnp.int32)[None, :, None]
    third_pos = jnp.arange(NZ, dtype=jnp.int32)[None, None, :]
    slab_number = (first_pos + second_pos + third_pos) // slab_width % 3
    members = jnp.arange(3, dtype=jnp.int32)[:, None, None, None]
    strong = slab_number[None] == members
    diffusion_low = jnp.where(strong, jnp.float32(16.0), jnp.float32(0.15))
    diffusion_high = jnp.where(strong, jnp.float32(32.0), jnp.float32(0.3))
    reaction_low = jnp.full((1, NX, NY, NZ), 0.1, jnp.float32)
    reaction_high = jnp.full((1, NX, NY, NZ), 1.0, jnp.float32)
    lowest = jnp.concatenate([diffusion_low, reaction_low], 0)
    highest = jnp.concatenate([diffusion_high, reaction_high], 0)
    uniform_draw = jax.random.uniform(jax.random.fold_in(key, 11), (4, NX, NY, NZ), jnp.float32)
    return lowest * jnp.exp(uniform_draw * jnp.log(highest / lowest))


def draw_right_side(key, part):
    noise = jax.random.normal(jax.random.fold_in(key, 23), (NX, NY, NZ), jnp.float32)
    return jnp.clip(noise, -5.0, 5.0)


def steps_of(key, extent, shards, low, top_value):
    factor_of, own = 1.0, jax.random.fold_in(key, 6)
    for position, shards_of in shards:
        draws = jnp.exp(jax.random.uniform(jax.random.fold_in(own, position), (shards_of,), jnp.float32, low / len(shards), top_value / len(shards)))
        factor_of = factor_of * jnp.repeat(draws, extent[position] // shards_of).reshape([-1 if axis == position else 1 for axis in range(len(extent))])
    return factor_of


def scatter_about(stream_key, dims, width, reach, pieces=(), held_as=jnp.bfloat16):
    values = jax.random.normal(stream_key, dims, jnp.float32) * width
    if len(pieces) > 0:
        values = steps_of(stream_key, dims, pieces, -0.22, 0.18) * values
    return jnp.clip(values, min=-reach, max=reach).astype(held_as)


def setup_inputs(seed: int = 0) -> dict:
    streams_of = jax.random.split(jax.random.key(seed), 4)
    right_side = draw_right_side(jax.random.fold_in(streams_of[3], 71), 0)
    coefficients = draw_coefficients(jax.random.fold_in(streams_of[3], 71), 0)
    first_guess = scatter_about(streams_of[2], (NX, NY, NZ), 0.5, 3.0, ((0, 2), (1, 4), (2, 4)), jnp.float32)
    return {"right_side": right_side, "coefficients": coefficients, "first_guess": first_guess}


relaxation = 0.8
blending = 0.4


def pad_along(values, direction):
    widths = [(0, 0)] * values.ndim
    widths[direction] = (1, 1)
    return jnp.pad(values, widths)


def neighbours(values, direction):
    length = values.shape[direction]
    padded = pad_along(values, direction)
    upper_cells = lax.slice_in_dim(padded, 2, length + 2, axis=direction)
    lower_cells = lax.slice_in_dim(padded, 0, length, axis=direction)
    return upper_cells, lower_cells


def face_weights(fields):
    diagonal = fields[3]
    weights = []
    for direction in range(3):
        upper_cells, lower_cells = neighbours(fields[direction], direction)
        weight_high = 0.5 * (fields[direction] + upper_cells)
        weight_low = 0.5 * (fields[direction] + lower_cells)
        weights.append((weight_high, weight_low))
        diagonal = diagonal + weight_high + weight_low
    return weights, diagonal


def operate(values, reaction, weights):
    result = reaction * values
    for direction in range(3):
        weight_high, weight_low = weights[direction]
        upper_cells, lower_cells = neighbours(values, direction)
        result = result + (weight_high * (values - upper_cells) + weight_low * (values - lower_cells))
    return result


def pair_mean(values, direction):
    shape = values.shape
    split_shape = shape[:direction] + (shape[direction] // 2, 2) + shape[direction + 1:]
    paired = values.reshape(split_shape)
    even_cells = lax.index_in_dim(paired, 0, direction + 1, keepdims=False)
    odd_cells = lax.index_in_dim(paired, 1, direction + 1, keepdims=False)
    return 0.5 * (even_cells + odd_cells)


def coarse_fields(fields, direction):
    averaged = pair_mean(fields, direction + 1)
    factors = [1.0, 1.0, 1.0, 1.0]
    factors[direction] = 0.25
    return jnp.stack([averaged[member] * factors[member] for member in range(4)])


def prolong_padded(padded, direction):
    length = padded.shape[direction] - 2
    middle = lax.slice_in_dim(padded, 1, length + 1, axis=direction)
    upper_cells = lax.slice_in_dim(padded, 2, length + 2, axis=direction)
    lower_cells = lax.slice_in_dim(padded, 0, length, axis=direction)
    even_cells = 0.75 * middle + 0.25 * lower_cells
    odd_cells = 0.75 * middle + 0.25 * upper_cells
    joined = jnp.stack([even_cells, odd_cells], direction + 1)
    new_shape = list(middle.shape)
    new_shape[direction] = 2 * length
    return joined.reshape(new_shape)


def reference(right_side, coefficients, first_guess):
    weights, diagonal = face_weights(coefficients)
    branches = []
    for direction in range(3):
        coarse = coarse_fields(coefficients, direction)
        coarse_weights, coarse_diagonal = face_weights(coarse)
        branches.append((coarse[3], coarse_weights, coarse_diagonal))
    solution_field = first_guess
    for cycle_index in range(CYCLES):
        residual = right_side - operate(solution_field, coefficients[3], weights)
        update = None
        for direction in range(3):
            coarse_reaction, coarse_weights, coarse_diagonal = branches[direction]
            coarse_residual = pair_mean(residual, direction)
            errors = jnp.zeros_like(coarse_residual)
            for repeat in range(SWEEPS):
                errors = errors + relaxation * (coarse_residual - operate(errors, coarse_reaction, coarse_weights)) / coarse_diagonal
            correction = prolong_padded(pad_along(errors, direction), direction)
            update = correction if update is None else update + correction
        solution_field = solution_field + blending * update
    return solution_field
```

```python
import functools

import jax
import jax.numpy as jnp
from jax import lax
from jax.experimental import pallas as pl
from jax.experimental.pallas import tpu as pltpu
from jax.sharding import PartitionSpec as P

CYCLES = 2
SWEEPS = 8
REACH = 2 * (SWEEPS + 1)
STEP = 20
LANES = 128
CHUNK = 2

relaxation = 0.8
blending = 0.4
MESH = pl.DeviceIdType.MESH
HIGH = lax.Precision.HIGHEST


def iota(shape, dim):
    return lax.broadcasted_iota(jnp.int32, shape, dim)


def matmul(a, b):
    return lax.dot_general(
        a, b, (((1,), (0,)), ((), ())), precision=HIGH, preferred_element_type=jnp.float32
    )


def kernel(sizes, names, b_ref, k_ref, g_ref, out_ref, *scratch):
    (fields, weights, diag, es, yss, yrs, ms, fs, kxr, kys, kyr, zs, zr, us, ur,
     send, recv, ksend, krecv, zsend, zrecv) = scratch
    nx, ny, nz = sizes
    wide = nz + LANES
    shapes = ((nx // 2, ny, wide), (nx, ny // 2, wide), (nx, ny, nz // 2 + LANES), (nx, ny, wide))
    place = [lax.axis_index(n) for n in names]
    counts = [lax.axis_size(n) for n in names]
    has_low = [p > 0 for p in place]
    has_high = [p < c - 1 for p, c in zip(place, counts)]
    ways = []
    for axis in range(3):
        ways.append((axis, -1, has_low[axis], has_high[axis]))
        ways.append((axis, 1, has_high[axis], has_low[axis]))

    def target(way):
        axis, step = ways[way][:2]
        return {names[axis]: place[axis] + step}

    def copy(src, dst, ssem, rsem, way):
        return pltpu.make_async_remote_copy(
            src_ref=src, dst_ref=dst, send_sem=ssem, recv_sem=rsem,
            device_id=target(way), device_id_type=MESH,
        )

    def start(copies):
        for way, c in copies:
            @pl.when(ways[way][2])
            def _():
                c.start()

    def finish(copies):
        for way, c in copies:
            @pl.when(ways[way][3])
            def _():
                c.wait_recv()
        for way, c in copies:
            @pl.when(ways[way][2])
            def _():
                c.wait_send()

    def faces(g, slot):
        x = shapes[g][0]
        e, ys, yr = es[g], yss[g], yrs[g]
        return [
            (0, copy(e.at[slot, 1], e.at[slot, x + 1], send.at[g, 0, slot], recv.at[g, 0, slot], 0)),
            (1, copy(e.at[slot, x], e.at[slot, 0], send.at[g, 1, slot], recv.at[g, 1, slot], 1)),
            (2, copy(ys.at[slot, 0], yr.at[slot, 1], send.at[g, 2, slot], recv.at[g, 2, slot], 2)),
            (3, copy(ys.at[slot, 1], yr.at[slot, 0], send.at[g, 3, slot], recv.at[g, 3, slot], 3)),
        ]

    for g in range(4):
        x = shapes[g][0]
        for slot in range(2):
            zero = jnp.zeros(shapes[g][1:], jnp.float32)
            es[g][slot, 0] = zero
            es[g][slot, x + 1] = zero
        yrs[g][...] = jnp.zeros(yrs[g].shape, jnp.float32)
    kxr[...] = jnp.zeros(kxr.shape, jnp.float32)
    kyr[...] = jnp.zeros(kyr.shape, jnp.float32)
    zr[...] = jnp.zeros(zr.shape, jnp.float32)
    ur[...] = jnp.zeros(ur.shape, jnp.float32)

    barrier = pltpu.get_barrier_semaphore()
    for way in range(6):
        @pl.when(ways[way][2])
        def _():
            pl.semaphore_signal(barrier, inc=1, device_id=target(way), device_id_type=MESH)
    peers = sum(jnp.where(has, 1, 0) for has in has_low + has_high)
    pl.semaphore_wait(barrier, peers)

    lane = iota((nx, ny, LANES), 2)
    low = jnp.zeros((nx, ny, LANES), jnp.float32)
    high = low
    for j in range(6):
        if j < 4:
            first, last = k_ref[j, :, :, :LANES], k_ref[j, :, :, nz - LANES:]
        elif j == 4:
            first, last = g_ref[:, :, :LANES], g_ref[:, :, nz - LANES:]
        else:
            first, last = b_ref[:, :, :LANES], b_ref[:, :, nz - LANES:]
        here = (lane >= STEP * j) & (lane < STEP * j + REACH)
        low = jnp.where(here, pltpu.roll(first, STEP * j, 2) if j else first, low)
        high = jnp.where(here, pltpu.roll(last, (STEP * j + REACH) % LANES, 2), high)
    zs[0] = low
    zs[1] = high
    deep = [
        (4, copy(zs.at[0], zr.at[1], zsend.at[0], zrecv.at[0], 4)),
        (5, copy(zs.at[1], zr.at[0], zsend.at[1], zrecv.at[1], 5)),
    ]
    start(deep)
    for j in range(4):
        fields[j, :, :, :nz] = k_ref[j]
    fields[4, :, :, :nz] = b_ref[...]
    es[3][0, 1:nx + 1, :, :nz] = g_ref[...]
    finish(deep)
    above, below = zr[1], zr[0]

    def beside(j):
        up = pltpu.roll(above, (LANES - STEP * j) % LANES, 2) if j else above
        down = pltpu.roll(below, (2 * LANES - REACH - STEP * j) % LANES, 2)
        return jnp.where(lane < REACH, up, jnp.where(lane >= LANES - REACH, down, 0.0))

    for j in range(4):
        fields[j, :, :, nz:] = beside(j)
    es[3][0, 1:nx + 1, :, nz:] = beside(4)
    fields[4, :, :, nz:] = beside(5)

    def send_guess(slot):
        u = es[3][slot, 1:nx + 1]
        yss[3][slot, 0] = u[:, 0:1, :]
        yss[3][slot, 1] = u[:, ny - 1:ny, :]
        start(faces(3, slot))

    ky = fields[1]
    for row in range(2):
        kys[0, row] = ky[:, row:row + 1, :]
        kys[1, row] = ky[:, ny - 2 + row:ny - 1 + row, :]
    edges = [
        (0, copy(fields.at[0, pl.ds(0, 2)], kxr.at[1], ksend.at[0], krecv.at[0], 0)),
        (1, copy(fields.at[0, pl.ds(nx - 2, 2)], kxr.at[0], ksend.at[1], krecv.at[1], 1)),
        (2, copy(kys.at[0], kyr.at[1], ksend.at[2], krecv.at[2], 2)),
        (3, copy(kys.at[1], kyr.at[0], ksend.at[3], krecv.at[3], 3)),
    ]
    start(edges)
    send_guess(0)

    half = nz // 2
    r, c = iota((wide, half + LANES), 0), iota((wide, half + LANES), 1)
    home = jnp.where(
        r < nz, r // 2,
        jnp.where(r < nz + LANES // 2, half + (r - nz) // 2, half + LANES // 2 + (r - nz) // 2),
    )
    z_mean = jnp.where(home == c, 0.5, 0.0).astype(jnp.float32)
    rows = nx * ny
    r, c = iota((rows // 2, rows), 0), iota((rows // 2, rows), 1)
    y_mean = jnp.where(c // 2 == r, 0.5, 0.0).astype(jnp.float32)
    r, c = iota((rows, rows), 0), iota((rows, rows), 1)
    weave = jnp.where(r // 2 + (r % 2) * (rows // 2) == c, 1.0, 0.0).astype(jnp.float32)
    r, c = iota((half + LANES, nz), 0), iota((half + LANES, nz), 1)
    main = c // 2
    total = half + LANES
    side = jnp.where(c % 2 == 1, main + 1, jnp.where(main == 0, total - 1, main - 1))
    z_spread = (jnp.where(r == main, 0.75, 0.0) + jnp.where(r == side, 0.25, 0.0)).astype(jnp.float32)

    def mean(values, d):
        if d == 0:
            paired = values.reshape((values.shape[0] // 2, 2) + values.shape[1:])
            return 0.5 * (paired[:, 0] + paired[:, 1])
        flat = values.reshape((values.shape[0] * ny, wide))
        if d == 1:
            return matmul(y_mean, flat).reshape((nx, ny // 2, wide))
        return matmul(flat, z_mean).reshape(shapes[2])

    def y_shift(values, halo_low, halo_high):
        y = values.shape[1]
        row = iota(values.shape, 1)
        lower = jnp.where(row == 0, halo_low, pltpu.roll(values, 1, 1))
        upper = jnp.where(row == y - 1, halo_high, pltpu.roll(values, y - 1, 1))
        return lower, upper

    def z_shift(values):
        return pltpu.roll(values, 1, 2), pltpu.roll(values, values.shape[2] - 1, 2)

    def face_weights(k0, k1, k2, s, x_low, x_high, y_low, y_high):
        pairs = [
            (jnp.concatenate([x_low, k0[:-1]], 0), jnp.concatenate([k0[1:], x_high], 0)),
            y_shift(k1, y_low, y_high),
            z_shift(k2),
        ]
        found = []
        total = s
        for k, pair in zip((k0, k1, k2), pairs):
            for other in pair:
                w = 0.5 * (k + other)
                found.append(w)
                total = total + w
        return found, total

    finish(edges)
    near_x = (kxr[0, 1:2], kxr[1, 0:1])
    near_y = (kyr[0, 1], kyr[1, 0])
    w, total_fine = face_weights(
        fields[0], fields[1], fields[2], fields[3], *near_x, *near_y)
    for j in range(6):
        weights[j] = w[j]
    diag[...] = total_fine

    for d in range(3):
        coarse = [mean(fields[j], d) for j in range(4)]
        coarse[d] = coarse[d] * 0.25
        if d == 0:
            x_faces = [0.125 * (kxr[side, 0:1] + kxr[side, 1:2]) for side in range(2)]
            y_faces = [
                0.5 * (v[:, 0] + v[:, 1])
                for v in [h.reshape((nx // 2, 2, 1, wide)) for h in near_y]
            ]
        elif d == 1:
            x_faces = [
                matmul(y_mean[: ny // 2, :ny], v[0])[None] for v in near_x
            ]
            y_faces = [0.125 * (kyr[side, 0] + kyr[side, 1]) for side in range(2)]
        else:
            x_faces = [matmul(v[0], z_mean)[None] for v in near_x]
            y_faces = [
                jnp.stack([matmul(jnp.broadcast_to(v[i], (8, wide)), z_mean)[0:1] for i in range(nx)])
                for v in near_y
            ]
        w, total_coarse = face_weights(*coarse, *x_faces, *y_faces)
        inside = coarse[3] > 0.0
        scale = jnp.where(inside, relaxation / jnp.where(inside, total_coarse, 1.0), 0.0)
        ms[d][6] = scale
        for j in range(6):
            ms[d][j] = w[j] * scale

    def sweep(g, slot, new_slot):
        e, yr, ys, m, f = es[g], yrs[g], yss[g], ms[g], fs[g]
        x, y, z = shapes[g]
        for x0 in range(0, x, CHUNK):
            planes = slice(x0, x0 + CHUNK)
            middle = e[slot, x0 + 1:x0 + 1 + CHUNK]
            y_low, y_high = y_shift(middle, yr[slot, 0, planes], yr[slot, 1, planes])
            z_low, z_high = z_shift(middle)
            new = (1.0 - relaxation) * middle + f[planes]
            new = new + m[0, planes] * e[slot, x0:x0 + CHUNK]
            new = new + m[1, planes] * e[slot, x0 + 2:x0 + 2 + CHUNK]
            new = new + m[2, planes] * y_low
            new = new + m[3, planes] * y_high
            new = new + m[4, planes] * z_low
            new = new + m[5, planes] * z_high
            e[new_slot, x0 + 1:x0 + 1 + CHUNK] = new
            ys[new_slot, 0, planes] = new[:, 0:1]
            ys[new_slot, 1, planes] = new[:, y - 1:y]

    for cycle in range(CYCLES):
        slot = cycle % 2
        finish(faces(3, slot))
        u = es[3][slot]
        middle = u[1:nx + 1]
        y_low, y_high = y_shift(middle, yrs[3][slot, 0], yrs[3][slot, 1])
        z_low, z_high = z_shift(middle)
        residual = fields[4] - diag[...] * middle
        around = (u[0:nx], u[2:nx + 2], y_low, y_high, z_low, z_high)
        for j in range(6):
            residual = residual + weights[j] * around[j]
        for g in range(3):
            x, y, z = shapes[g]
            first = ms[g][6] * mean(residual, g)
            fs[g][...] = first
            es[g][1, 1:x + 1] = first
            yss[g][1, 0] = first[:, 0:1]
            yss[g][1, 1] = first[:, y - 1:y]
            start(faces(g, 1))

        @pl.loop(1, SWEEPS)
        def _(repeat):
            old = lax.rem(repeat, 2)
            for g in range(3):
                finish(faces(g, old))
                sweep(g, old, 1 - old)
                start(faces(g, 1 - old))

        last = SWEEPS % 2
        for g in range(3):
            finish(faces(g, last))
        e = es[0][last, :, :, :nz]
        x = nx // 2
        even = 0.75 * e[1:x + 1] + 0.25 * e[0:x]
        odd = 0.75 * e[1:x + 1] + 0.25 * e[2:x + 2]
        update = jnp.stack([even, odd], 1).reshape((nx, ny, nz))
        e = es[1][last, 1:nx + 1, :, :nz]
        y_low, y_high = y_shift(e, yrs[1][last, 0, :, :, :nz], yrs[1][last, 1, :, :, :nz])
        even = (0.75 * e + 0.25 * y_low).reshape((rows // 2, nz))
        odd = (0.75 * e + 0.25 * y_high).reshape((rows // 2, nz))
        update = update + matmul(weave, jnp.concatenate([even, odd], 0)).reshape((nx, ny, nz))
        e = es[2][last, 1:nx + 1].reshape((rows, half + LANES))
        update = update + matmul(e, z_spread).reshape((nx, ny, nz))
        result = es[3][slot, 1:nx + 1, :, :nz] + blending * update
        if cycle == CYCLES - 1:
            out_ref[...] = result
            continue
        per = LANES // STEP
        plane_lane = iota((ny, LANES), 1)
        groups = us.shape[1]
        for q in range(groups):
            low = jnp.zeros((ny, LANES), jnp.float32)
            high = low
            for p in range(min(per, nx - q * per)):
                plane = result[q * per + p]
                here = (plane_lane >= STEP * p) & (plane_lane < STEP * p + REACH)
                first = plane[:, :LANES]
                low = jnp.where(here, pltpu.roll(first, STEP * p, 1) if p else first, low)
                high = jnp.where(
                    here, pltpu.roll(plane[:, nz - LANES:], (STEP * p + REACH) % LANES, 1), high)
            us[0, q] = low
            us[1, q] = high
        again = [
            (4, copy(us.at[0], ur.at[1], zsend.at[2], zrecv.at[2], 4)),
            (5, copy(us.at[1], ur.at[0], zsend.at[3], zrecv.at[3], 5)),
        ]
        start(again)
        es[3][1 - slot, 1:nx + 1, :, :nz] = result
        finish(again)
        for i in range(nx):
            q, p = i // per, i % per
            up = pltpu.roll(ur[1, q], (LANES - STEP * p) % LANES, 1) if p else ur[1, q]
            down = pltpu.roll(ur[0, q], (2 * LANES - REACH - STEP * p) % LANES, 1)
            es[3][1 - slot, i + 1, :, nz:] = jnp.where(
                plane_lane < REACH, up, jnp.where(plane_lane >= LANES - REACH, down, 0.0))
        send_guess(1 - slot)


def body(names, right_side, coefficients, first_guess):
    nx, ny, nz = right_side.shape
    wide = nz + LANES
    shapes = ((nx // 2, ny, wide), (nx, ny // 2, wide), (nx, ny, nz // 2 + LANES), (nx, ny, wide))
    f32 = jnp.float32
    vmem = lambda *shape: pltpu.VMEM(shape, f32)
    dma = pltpu.SemaphoreType.DMA
    groups = -(-nx // (LANES // STEP))
    scratch = [
        vmem(5, nx, ny, wide),
        vmem(6, nx, ny, wide),
        vmem(nx, ny, wide),
        tuple(vmem(2, x + 2, y, z) for x, y, z in shapes),
        tuple(vmem(2, 2, x, 1, z) for x, y, z in shapes),
        tuple(vmem(2, 2, x, 1, z) for x, y, z in shapes),
        tuple(vmem(7, x, y, z) for x, y, z in shapes[:3]),
        tuple(vmem(x, y, z) for x, y, z in shapes[:3]),
        vmem(2, 2, ny, wide),
        vmem(2, 2, nx, 1, wide),
        vmem(2, 2, nx, 1, wide),
        vmem(2, nx, ny, LANES),
        vmem(2, nx, ny, LANES),
        vmem(2, groups, ny, LANES),
        vmem(2, groups, ny, LANES),
        dma((4, 4, 2)), dma((4, 4, 2)), dma((4,)), dma((4,)), dma((4,)), dma((4,)),
    ]
    spec = pl.BlockSpec(memory_space=pltpu.VMEM)
    return pl.pallas_call(
        functools.partial(kernel, (nx, ny, nz), names),
        out_shape=jax.ShapeDtypeStruct(right_side.shape, f32),
        in_specs=[spec] * 3,
        out_specs=spec,
        scratch_shapes=scratch,
        compiler_params=pltpu.CompilerParams(
            collective_id=0, has_side_effects=True, vmem_limit_bytes=60 * 1024 * 1024),
    )(right_side, coefficients, first_guess)


def solution(mesh):
    names = tuple(mesh.axis_names)
    in_specs = (P(*names), P(None, *names), P(*names))
    return jax.shard_map(
        functools.partial(body, names), mesh=mesh, in_specs=in_specs, out_specs=P(*names),
        check_vma=False)
```

```python
import functools

import jax
import jax.numpy as jnp
from jax import lax
from jax.experimental import pallas as pl
from jax.experimental.pallas import tpu as pltpu
from jax.sharding import PartitionSpec as P

CYCLES = 2
SWEEPS = 8
REACH = 2 * (SWEEPS + 1)
STEP = 20
LANES = 128
CHUNK = 2

relaxation = 0.8
blending = 0.4
MESH = pl.DeviceIdType.MESH


def iota(shape, dim):
    return lax.broadcasted_iota(jnp.int32, shape, dim)


def spread(a, b):
    total = None
    for _ in range(3):
        part = a.astype(jnp.bfloat16)
        a = a - part.astype(jnp.float32)
        term = jnp.dot(part, b, preferred_element_type=jnp.float32)
        total = term if total is None else total + term
    return total


def kernel(sizes, names, b_ref, k_ref, g_ref, out_ref, *scratch):
    (fields, cells, tiles, es, yss, yrs, ms, fs, kxr, kys, kyr, zs, zr, us, ur,
     send, recv, ksend, krecv, zsend, zrecv) = scratch
    nx, ny, nz = sizes
    wide = nz + LANES
    shapes = ((nx // 2, ny, wide), (nx, ny // 2, wide), (nx, ny, nz // 2 + LANES), (nx, ny, wide))
    place = [lax.axis_index(n) for n in names]
    counts = [lax.axis_size(n) for n in names]
    has_low = [p > 0 for p in place]
    has_high = [p < c - 1 for p, c in zip(place, counts)]
    ways = []
    for axis in range(3):
        ways.append((axis, -1, has_low[axis], has_high[axis]))
        ways.append((axis, 1, has_high[axis], has_low[axis]))

    def target(way):
        axis, step = ways[way][:2]
        return {names[axis]: place[axis] + step}

    def copy(src, dst, ssem, rsem, way):
        return pltpu.make_async_remote_copy(
            src_ref=src, dst_ref=dst, send_sem=ssem, recv_sem=rsem,
            device_id=target(way), device_id_type=MESH,
        )

    def start(copies):
        for way, c in copies:
            @pl.when(ways[way][2])
            def _():
                c.start()

    def finish(copies):
        for way, c in copies:
            @pl.when(ways[way][3])
            def _():
                c.wait_recv()
        for way, c in copies:
            @pl.when(ways[way][2])
            def _():
                c.wait_send()

    def faces(g, slot):
        x = shapes[g][0]
        e, ys, yr = es[g], yss[g], yrs[g]
        return [
            (0, copy(e.at[slot, 1], e.at[slot, x + 1], send.at[g, 0, slot], recv.at[g, 0, slot], 0)),
            (1, copy(e.at[slot, x], e.at[slot, 0], send.at[g, 1, slot], recv.at[g, 1, slot], 1)),
            (2, copy(ys.at[slot, 0], yr.at[slot, 1], send.at[g, 2, slot], recv.at[g, 2, slot], 2)),
            (3, copy(ys.at[slot, 1], yr.at[slot, 0], send.at[g, 3, slot], recv.at[g, 3, slot], 3)),
        ]

    for g in range(4):
        x = shapes[g][0]
        for slot in range(2):
            zero = jnp.zeros(shapes[g][1:], jnp.float32)
            es[g][slot, 0] = zero
            es[g][slot, x + 1] = zero
        yrs[g][...] = jnp.zeros(yrs[g].shape, jnp.float32)
    kxr[...] = jnp.zeros(kxr.shape, jnp.float32)
    kyr[...] = jnp.zeros(kyr.shape, jnp.float32)
    zr[...] = jnp.zeros(zr.shape, jnp.float32)
    ur[...] = jnp.zeros(ur.shape, jnp.float32)

    barrier = pltpu.get_barrier_semaphore()
    for way in range(6):
        @pl.when(ways[way][2])
        def _():
            pl.semaphore_signal(barrier, inc=1, device_id=target(way), device_id_type=MESH)
    peers = sum(jnp.where(has, 1, 0) for has in has_low + has_high)
    pl.semaphore_wait(barrier, peers)

    lane = iota((nx, ny, LANES), 2)
    low = jnp.zeros((nx, ny, LANES), jnp.float32)
    high = low
    for j in range(6):
        if j < 4:
            first, last = k_ref[j, :, :, :LANES], k_ref[j, :, :, nz - LANES:]
        elif j == 4:
            first, last = g_ref[:, :, :LANES], g_ref[:, :, nz - LANES:]
        else:
            first, last = b_ref[:, :, :LANES], b_ref[:, :, nz - LANES:]
        here = (lane >= STEP * j) & (lane < STEP * j + REACH)
        low = jnp.where(here, pltpu.roll(first, STEP * j, 2) if j else first, low)
        high = jnp.where(here, pltpu.roll(last, (STEP * j + REACH) % LANES, 2), high)
    zs[0] = low
    zs[1] = high
    deep = [
        (4, copy(zs.at[0], zr.at[1], zsend.at[0], zrecv.at[0], 4)),
        (5, copy(zs.at[1], zr.at[0], zsend.at[1], zrecv.at[1], 5)),
    ]
    start(deep)
    for j in range(4):
        fields[j, :, :, :nz] = k_ref[j]
    fields[4, :, :, :nz] = b_ref[...]
    es[3][0, 1:nx + 1, :, :nz] = g_ref[...]
    finish(deep)
    above, below = zr[1], zr[0]

    def beside(j):
        up = pltpu.roll(above, (LANES - STEP * j) % LANES, 2) if j else above
        down = pltpu.roll(below, (2 * LANES - REACH - STEP * j) % LANES, 2)
        return jnp.where(lane < REACH, up, jnp.where(lane >= LANES - REACH, down, 0.0))

    for j in range(4):
        fields[j, :, :, nz:] = beside(j)
    es[3][0, 1:nx + 1, :, nz:] = beside(4)
    fields[4, :, :, nz:] = beside(5)

    def send_guess(slot):
        u = es[3][slot, 1:nx + 1]
        yss[3][slot, 0] = u[:, 0:1, :]
        yss[3][slot, 1] = u[:, ny - 1:ny, :]
        start(faces(3, slot))

    ky = fields[1]
    for row in range(2):
        kys[0, row] = ky[:, row:row + 1, :]
        kys[1, row] = ky[:, ny - 2 + row:ny - 1 + row, :]
    edges = [
        (0, copy(fields.at[0, pl.ds(0, 2)], kxr.at[1], ksend.at[0], krecv.at[0], 0)),
        (1, copy(fields.at[0, pl.ds(nx - 2, 2)], kxr.at[0], ksend.at[1], krecv.at[1], 1)),
        (2, copy(kys.at[0], kyr.at[1], ksend.at[2], krecv.at[2], 2)),
        (3, copy(kys.at[1], kyr.at[0], ksend.at[3], krecv.at[3], 3)),
    ]
    start(edges)
    send_guess(0)

    half = nz // 2
    r, c = iota((wide, half + LANES), 0), iota((wide, half + LANES), 1)
    home = jnp.where(
        r < nz, r // 2,
        jnp.where(r < nz + LANES // 2, half + (r - nz) // 2, half + LANES // 2 + (r - nz) // 2),
    )
    z_mean = jnp.where(home == c, 0.5, 0.0).astype(jnp.bfloat16)
    rows = nx * ny
    r, c = iota((half + LANES, nz), 0), iota((half + LANES, nz), 1)
    main = c // 2
    total = half + LANES
    side = jnp.where(c % 2 == 1, main + 1, jnp.where(main == 0, total - 1, main - 1))
    z_spread = (jnp.where(r == main, 0.75, 0.0) + jnp.where(r == side, 0.25, 0.0)).astype(jnp.bfloat16)

    count = wide // LANES
    even_rows, odd_rows = pl.ds(0, ny // 2, stride=2), pl.ds(1, ny // 2, stride=2)

    def put_tiles(planes, values):
        for t in range(values.shape[2] // LANES):
            tiles[t, planes] = values[:, :, LANES * t:LANES * (t + 1)]

    def get_tiles(planes, tiles_of=count):
        return jnp.concatenate([tiles[t, planes] for t in range(tiles_of)], 2)

    def y_mean(planes):
        return jnp.concatenate(
            [0.5 * (tiles[t, planes, even_rows] + tiles[t, planes, odd_rows]) for t in range(count)], 2)

    def chunks(x, step=CHUNK):
        return [slice(x0, x0 + step) for x0 in range(0, x, step)]

    def below_of(ref, planes, halo):
        if planes.start > 0:
            return ref[planes.start - 1:planes.stop - 1]
        return jnp.concatenate([halo, ref[0:planes.stop - 1]], 0)

    def above_of(ref, planes, halo):
        if planes.stop < ref.shape[0]:
            return ref[planes.start + 1:planes.stop + 1]
        return jnp.concatenate([ref[planes.start + 1:planes.stop], halo], 0)

    def y_shift(values, halo_low, halo_high):
        y = values.shape[1]
        row = iota(values.shape, 1)
        lower = jnp.where(row == 0, halo_low, pltpu.roll(values, 1, 1))
        upper = jnp.where(row == y - 1, halo_high, pltpu.roll(values, y - 1, 1))
        return lower, upper

    def z_shift(values):
        return pltpu.roll(values, 1, 2), pltpu.roll(values, values.shape[2] - 1, 2)

    def face_weights(k, planes, near_x, near_y):
        k0, k1, k2 = k.at[0], k.at[1], k.at[2]
        m1, m2 = k1[planes], k2[planes]
        groups = (
            (k0[planes], (below_of(k0, planes, near_x[0]), above_of(k0, planes, near_x[1]))),
            (m1, y_shift(m1, near_y[0](planes), near_y[1](planes))),
            (m2, z_shift(m2)),
        )
        found = []
        total = k[3, planes]
        for middle, pair in groups:
            for other in pair:
                found.append(0.5 * (middle + other))
                total = total + found[-1]
        return found, total

    for j in range(4):
        for d in range(2):
            factor = 0.25 if j == d else 1.0
            if d == 0:
                for i in range(nx // 2):
                    cells[0][j, i] = (0.5 * factor) * (fields[j, 2 * i] + fields[j, 2 * i + 1])
            else:
                for planes in chunks(nx):
                    put_tiles(planes, fields[j, planes])
                for planes in chunks(nx):
                    cells[1][j, planes] = y_mean(planes) * factor
    finish(edges)
    near_rows = [kxr[0, 1], kxr[1, 0]] + [kyr[0, 1].reshape((nx, wide)), kyr[1, 0].reshape((nx, wide))]
    flat = jnp.concatenate([fields[j].reshape((rows, wide)) for j in range(4)] + near_rows, 0)
    flat = spread(flat, z_mean)
    for j in range(4):
        part = flat[rows * j:rows * (j + 1)] * (0.25 if j == 2 else 1.0)
        cells[2][j] = part.reshape(shapes[2])
    edge = flat[4 * rows:]
    edge_x = [edge[0:ny][None], edge[ny:2 * ny][None]]
    edge_y = [edge[2 * ny + nx * side:2 * ny + nx * (side + 1)].reshape((nx, 1, half + LANES)) for side in range(2)]
    put_tiles(slice(0, 2), jnp.stack([kxr[0, 1], kxr[1, 0]]))
    pair = y_mean(slice(0, 2))

    near_xs = (
        [0.125 * (kxr[side, 0:1] + kxr[side, 1:2]) for side in range(2)],
        [pair[0:1], pair[1:2]],
        edge_x,
    )

    def y_face(d, side):
        nearest = kyr.at[side, 1 - side]
        if d == 0:
            return lambda planes: jnp.concatenate(
                [0.5 * (nearest[2 * i:2 * i + 1] + nearest[2 * i + 1:2 * i + 2])
                 for i in range(planes.start, planes.stop)], 0)
        if d == 1:
            return lambda planes: 0.125 * (kyr[side, 0, planes] + kyr[side, 1, planes])
        if d == 2:
            return lambda planes: edge_y[side][planes]
        return lambda planes: nearest[planes]

    for d in range(3):
        for planes in chunks(shapes[d][0]):
            w, total_coarse = face_weights(
                cells[d], planes, near_xs[d], (y_face(d, 0), y_face(d, 1)))
            inside = cells[d][3, planes] > 0.0
            scale = jnp.where(inside, relaxation / jnp.where(inside, total_coarse, 1.0), 0.0)
            ms[d][6, planes] = scale
            for j in range(6):
                ms[d][j, planes] = w[j] * scale

    def sweep(g, slot, new_slot):
        e, yr, ys, m, f = es[g], yrs[g], yss[g], ms[g], fs[g]
        x, y, z = shapes[g]
        for x0 in range(0, x, CHUNK):
            planes = slice(x0, x0 + CHUNK)
            middle = e[slot, x0 + 1:x0 + 1 + CHUNK]
            y_low, y_high = y_shift(middle, yr[slot, 0, planes], yr[slot, 1, planes])
            z_low, z_high = z_shift(middle)
            new = (1.0 - relaxation) * middle + f[planes]
            new = new + m[0, planes] * e[slot, x0:x0 + CHUNK]
            new = new + m[1, planes] * e[slot, x0 + 2:x0 + 2 + CHUNK]
            new = new + m[2, planes] * y_low
            new = new + m[3, planes] * y_high
            new = new + m[4, planes] * z_low
            new = new + m[5, planes] * z_high
            e[new_slot, x0 + 1:x0 + 1 + CHUNK] = new
            ys[new_slot, 0, planes] = new[:, 0:1]
            ys[new_slot, 1, planes] = new[:, y - 1:y]

    for cycle in range(CYCLES):
        slot = cycle % 2
        finish(faces(3, slot))
        u = es[3]
        for planes in chunks(nx):
            x0, x1 = planes.start, planes.stop
            middle = u[slot, x0 + 1:x1 + 1]
            y_low, y_high = y_shift(middle, yrs[3][slot, 0, planes], yrs[3][slot, 1, planes])
            z_low, z_high = z_shift(middle)
            w, total_fine = face_weights(
                fields, planes, (kxr[0, 1:2], kxr[1, 0:1]), (y_face(3, 0), y_face(3, 1)))
            residual = fields[4, planes] - total_fine * middle
            around = (u[slot, x0:x1], u[slot, x0 + 2:x1 + 2], y_low, y_high, z_low, z_high)
            for j in range(6):
                residual = residual + w[j] * around[j]
            put_tiles(planes, residual)
        for g in range(3):
            x, y, z = shapes[g]
            if g == 2:
                flat = get_tiles(slice(0, nx)).reshape((rows, wide))
                whole = spread(flat, z_mean).reshape(shapes[2])
            for planes in chunks(x):
                if g == 0:
                    pairs = [get_tiles(slice(2 * i, 2 * i + 2)) for i in range(planes.start, planes.stop)]
                    first = jnp.concatenate([0.5 * (p[0:1] + p[1:2]) for p in pairs], 0)
                elif g == 1:
                    first = y_mean(planes)
                else:
                    first = whole[planes]
                first = ms[g][6, planes] * first
                fs[g][planes] = first
                es[g][1, planes.start + 1:planes.stop + 1] = first
                yss[g][1, 0, planes] = first[:, 0:1]
                yss[g][1, 1, planes] = first[:, y - 1:y]
            start(faces(g, 1))

        @pl.loop(1, SWEEPS)
        def _(repeat):
            old = lax.rem(repeat, 2)
            for g in range(3):
                finish(faces(g, old))
                sweep(g, old, 1 - old)
                start(faces(g, 1 - old))

        last = SWEEPS % 2
        for g in range(3):
            finish(faces(g, last))
        e = es[2][last, 1:nx + 1].reshape((rows, half + LANES))
        from_z = spread(e, z_spread).reshape((nx, ny, nz))
        for planes in chunks(nx):
            e = es[1][last, planes.start + 1:planes.stop + 1, :, :nz]
            y_low, y_high = y_shift(
                e, yrs[1][last, 0, planes, :, :nz], yrs[1][last, 1, planes, :, :nz])
            even = 0.75 * e + 0.25 * y_low
            odd = 0.75 * e + 0.25 * y_high
            for t in range(nz // LANES):
                tiles[t, planes, even_rows] = even[:, :, LANES * t:LANES * (t + 1)]
                tiles[t, planes, odd_rows] = odd[:, :, LANES * t:LANES * (t + 1)]
        for i in range(nx // 2):
            planes = slice(2 * i, 2 * i + 2)
            e = es[0][last, i:i + 3, :, :nz]
            even = 0.75 * e[1:2] + 0.25 * e[0:1]
            odd = 0.75 * e[1:2] + 0.25 * e[2:3]
            update = (jnp.concatenate([even, odd], 0) + get_tiles(planes, nz // LANES)) + from_z[planes]
            final = es[3][slot, 2 * i + 1:2 * i + 3, :, :nz] + blending * update
            if cycle == CYCLES - 1:
                out_ref[planes] = final
            else:
                es[3][1 - slot, 2 * i + 1:2 * i + 3, :, :nz] = final
        if cycle == CYCLES - 1:
            continue
        result = es[3].at[1 - slot, 1:nx + 1]
        per = LANES // STEP
        plane_lane = iota((ny, LANES), 1)
        groups = us.shape[1]
        for q in range(groups):
            low = jnp.zeros((ny, LANES), jnp.float32)
            high = low
            for p in range(min(per, nx - q * per)):
                here = (plane_lane >= STEP * p) & (plane_lane < STEP * p + REACH)
                first = result[q * per + p, :, :LANES]
                low = jnp.where(here, pltpu.roll(first, STEP * p, 1) if p else first, low)
                high = jnp.where(
                    here, pltpu.roll(result[q * per + p, :, nz - LANES:nz], (STEP * p + REACH) % LANES, 1), high)
            us[0, q] = low
            us[1, q] = high
        again = [
            (4, copy(us.at[0], ur.at[1], zsend.at[2], zrecv.at[2], 4)),
            (5, copy(us.at[1], ur.at[0], zsend.at[3], zrecv.at[3], 5)),
        ]
        start(again)
        finish(again)
        for i in range(nx):
            q, p = i // per, i % per
            up = pltpu.roll(ur[1, q], (LANES - STEP * p) % LANES, 1) if p else ur[1, q]
            down = pltpu.roll(ur[0, q], (2 * LANES - REACH - STEP * p) % LANES, 1)
            es[3][1 - slot, i + 1, :, nz:] = jnp.where(
                plane_lane < REACH, up, jnp.where(plane_lane >= LANES - REACH, down, 0.0))
        send_guess(1 - slot)


def body(names, right_side, coefficients, first_guess):
    nx, ny, nz = right_side.shape
    wide = nz + LANES
    shapes = ((nx // 2, ny, wide), (nx, ny // 2, wide), (nx, ny, nz // 2 + LANES), (nx, ny, wide))
    f32 = jnp.float32
    vmem = lambda *shape: pltpu.VMEM(shape, f32)
    dma = pltpu.SemaphoreType.DMA
    groups = -(-nx // (LANES // STEP))
    scratch = [
        vmem(5, nx, ny, wide),
        tuple(vmem(4, x, y, z) for x, y, z in shapes[:3]),
        vmem(wide // LANES, nx, ny, LANES),
        tuple(vmem(2, x + 2, y, z) for x, y, z in shapes),
        tuple(vmem(2, 2, x, 1, z) for x, y, z in shapes),
        tuple(vmem(2, 2, x, 1, z) for x, y, z in shapes),
        tuple(vmem(7, x, y, z) for x, y, z in shapes[:3]),
        tuple(vmem(x, y, z) for x, y, z in shapes[:3]),
        vmem(2, 2, ny, wide),
        vmem(2, 2, nx, 1, wide),
        vmem(2, 2, nx, 1, wide),
        vmem(2, nx, ny, LANES),
        vmem(2, nx, ny, LANES),
        vmem(2, groups, ny, LANES),
        vmem(2, groups, ny, LANES),
        dma((4, 4, 2)), dma((4, 4, 2)), dma((4,)), dma((4,)), dma((4,)), dma((4,)),
    ]
    spec = pl.BlockSpec(memory_space=pltpu.VMEM)
    return pl.pallas_call(
        functools.partial(kernel, (nx, ny, nz), names),
        out_shape=jax.ShapeDtypeStruct(right_side.shape, f32),
        in_specs=[spec] * 3,
        out_specs=spec,
        scratch_shapes=scratch,
        compiler_params=pltpu.CompilerParams(
            collective_id=0, has_side_effects=True, vmem_limit_bytes=60 * 1024 * 1024),
    )(right_side, coefficients, first_guess)


def solution(mesh):
    names = tuple(mesh.axis_names)
    in_specs = (P(*names), P(None, *names), P(*names))
    return jax.shard_map(
        functools.partial(body, names), mesh=mesh, in_specs=in_specs, out_specs=P(*names),
        check_vma=False)
```

```python
import functools

import jax
import jax.numpy as jnp
from jax import lax
from jax.experimental import pallas as pl
from jax.experimental.pallas import tpu as pltpu
from jax.sharding import PartitionSpec as P

CYCLES = 2
SWEEPS = 8
REACH = 2 * (SWEEPS + 1)
STEP = 20
LANES = 128
CHUNK = 2

relaxation = 0.8
blending = 0.4
MESH = pl.DeviceIdType.MESH


def iota(shape, dim):
    return lax.broadcasted_iota(jnp.int32, shape, dim)


def spread(a, b):
    total = None
    for _ in range(3):
        part = a.astype(jnp.bfloat16)
        a = a - part.astype(jnp.float32)
        term = jnp.dot(part, b, preferred_element_type=jnp.float32)
        total = term if total is None else total + term
    return total


def kernel(sizes, names, b_ref, k_ref, g_ref, out_ref, *scratch):
    (fields, cells, tiles, es, yss, yrs, ms, fs, kxr, kys, kyr, zs, zr, us, ur,
     send, recv, ksend, krecv, zsend, zrecv) = scratch
    nx, ny, nz = sizes
    wide = nz + LANES
    shapes = ((nx // 2, ny, wide), (nx, ny // 2, wide), (nx, ny, nz // 2 + LANES), (nx, ny, wide))
    place = [lax.axis_index(n) for n in names]
    counts = [lax.axis_size(n) for n in names]
    has_low = [p > 0 for p in place]
    has_high = [p < c - 1 for p, c in zip(place, counts)]
    ways = []
    for axis in range(3):
        ways.append((axis, -1, has_low[axis], has_high[axis]))
        ways.append((axis, 1, has_high[axis], has_low[axis]))

    def target(way):
        axis, step = ways[way][:2]
        return {names[axis]: place[axis] + step}

    def copy(src, dst, ssem, rsem, way):
        return pltpu.make_async_remote_copy(
            src_ref=src, dst_ref=dst, send_sem=ssem, recv_sem=rsem,
            device_id=target(way), device_id_type=MESH,
        )

    def start(copies):
        for way, c in copies:
            @pl.when(ways[way][2])
            def _():
                c.start()

    def finish(copies):
        for way, c in copies:
            @pl.when(ways[way][3])
            def _():
                c.wait_recv()
        for way, c in copies:
            @pl.when(ways[way][2])
            def _():
                c.wait_send()

    def faces(g, slot, keep=(0, 1, 2, 3)):
        x = shapes[g][0]
        e, ys, yr = es[g], yss[g], yrs[g]
        ends = (
            (e.at[slot, 1], e.at[slot, x + 1]),
            (e.at[slot, x], e.at[slot, 0]),
            (ys.at[slot, 0], yr.at[slot, 1]),
            (ys.at[slot, 1], yr.at[slot, 0]),
        )
        return [
            (way, copy(*ends[way], send.at[g, way, slot], recv.at[g, way, slot], way)) for way in keep
        ]

    for g in range(4):
        x = shapes[g][0]
        for slot in range(2):
            zero = jnp.zeros(shapes[g][1:], jnp.float32)
            es[g][slot, 0] = zero
            es[g][slot, x + 1] = zero
        yrs[g][...] = jnp.zeros(yrs[g].shape, jnp.float32)
    kxr[...] = jnp.zeros(kxr.shape, jnp.float32)
    kyr[...] = jnp.zeros(kyr.shape, jnp.float32)
    zr[...] = jnp.zeros(zr.shape, jnp.float32)
    ur[...] = jnp.zeros(ur.shape, jnp.float32)

    barrier = pltpu.get_barrier_semaphore()
    for way in range(6):
        @pl.when(ways[way][2])
        def _():
            pl.semaphore_signal(barrier, inc=1, device_id=target(way), device_id_type=MESH)
    peers = sum(jnp.where(has, 1, 0) for has in has_low + has_high)
    pl.semaphore_wait(barrier, peers)

    lane = iota((nx, ny, LANES), 2)
    low = jnp.zeros((nx, ny, LANES), jnp.float32)
    high = low
    for j in range(6):
        if j < 4:
            first, last = k_ref[j, :, :, :LANES], k_ref[j, :, :, nz - LANES:]
        elif j == 4:
            first, last = g_ref[:, :, :LANES], g_ref[:, :, nz - LANES:]
        else:
            first, last = b_ref[:, :, :LANES], b_ref[:, :, nz - LANES:]
        here = (lane >= STEP * j) & (lane < STEP * j + REACH)
        low = jnp.where(here, pltpu.roll(first, STEP * j, 2) if j else first, low)
        high = jnp.where(here, pltpu.roll(last, (STEP * j + REACH) % LANES, 2), high)
    zs[0] = low
    zs[1] = high
    deep = [
        (4, copy(zs.at[0], zr.at[1], zsend.at[0], zrecv.at[0], 4)),
        (5, copy(zs.at[1], zr.at[0], zsend.at[1], zrecv.at[1], 5)),
    ]
    start(deep)
    for j in range(4):
        fields[j, :, :, :nz] = k_ref[j]
    fields[4, :, :, :nz] = b_ref[...]
    es[3][0, 1:nx + 1, :, :nz] = g_ref[...]
    finish(deep)
    above, below = zr[1], zr[0]

    def beside(j):
        up = pltpu.roll(above, (LANES - STEP * j) % LANES, 2) if j else above
        down = pltpu.roll(below, (2 * LANES - REACH - STEP * j) % LANES, 2)
        return jnp.where(lane < REACH, up, jnp.where(lane >= LANES - REACH, down, 0.0))

    for j in range(4):
        fields[j, :, :, nz:] = beside(j)
    es[3][0, 1:nx + 1, :, nz:] = beside(4)
    fields[4, :, :, nz:] = beside(5)

    def send_guess(slot):
        u = es[3][slot, 1:nx + 1]
        yss[3][slot, 0] = u[:, 0:1, :]
        yss[3][slot, 1] = u[:, ny - 1:ny, :]
        start(faces(3, slot))

    ky = fields[1]
    for row in range(2):
        kys[0, row] = ky[:, row:row + 1, :]
        kys[1, row] = ky[:, ny - 2 + row:ny - 1 + row, :]
    edges = [
        (0, copy(fields.at[0, pl.ds(0, 2)], kxr.at[1], ksend.at[0], krecv.at[0], 0)),
        (1, copy(fields.at[0, pl.ds(nx - 2, 2)], kxr.at[0], ksend.at[1], krecv.at[1], 1)),
        (2, copy(kys.at[0], kyr.at[1], ksend.at[2], krecv.at[2], 2)),
        (3, copy(kys.at[1], kyr.at[0], ksend.at[3], krecv.at[3], 3)),
    ]
    start(edges)
    send_guess(0)

    half = nz // 2
    r, c = iota((wide, half + LANES), 0), iota((wide, half + LANES), 1)
    home = jnp.where(
        r < nz, r // 2,
        jnp.where(r < nz + LANES // 2, half + (r - nz) // 2, half + LANES // 2 + (r - nz) // 2),
    )
    z_mean = jnp.where(home == c, 0.5, 0.0).astype(jnp.bfloat16)
    rows = nx * ny
    r, c = iota((half + LANES, nz), 0), iota((half + LANES, nz), 1)
    main = c // 2
    total = half + LANES
    side = jnp.where(c % 2 == 1, main + 1, jnp.where(main == 0, total - 1, main - 1))
    z_spread = (jnp.where(r == main, 0.75, 0.0) + jnp.where(r == side, 0.25, 0.0)).astype(jnp.bfloat16)

    count = wide // LANES
    even_rows, odd_rows = pl.ds(0, ny // 2, stride=2), pl.ds(1, ny // 2, stride=2)

    def put_tiles(planes, values):
        for t in range(values.shape[2] // LANES):
            tiles[t, planes] = values[:, :, LANES * t:LANES * (t + 1)]

    def get_tiles(planes, tiles_of=count):
        return jnp.concatenate([tiles[t, planes] for t in range(tiles_of)], 2)

    def y_mean(planes):
        return jnp.concatenate(
            [0.5 * (tiles[t, planes, even_rows] + tiles[t, planes, odd_rows]) for t in range(count)], 2)

    def chunks(x, step=CHUNK):
        return [slice(x0, x0 + step) for x0 in range(0, x, step)]

    def below_of(ref, planes, halo):
        if planes.start > 0:
            return ref[planes.start - 1:planes.stop - 1]
        return jnp.concatenate([halo, ref[0:planes.stop - 1]], 0)

    def above_of(ref, planes, halo):
        if planes.stop < ref.shape[0]:
            return ref[planes.start + 1:planes.stop + 1]
        return jnp.concatenate([ref[planes.start + 1:planes.stop], halo], 0)

    def y_shift(values, halo_low, halo_high):
        y = values.shape[1]
        row = iota(values.shape, 1)
        lower = jnp.where(row == 0, halo_low, pltpu.roll(values, 1, 1))
        upper = jnp.where(row == y - 1, halo_high, pltpu.roll(values, y - 1, 1))
        return lower, upper

    def z_shift(values):
        return pltpu.roll(values, 1, 2), pltpu.roll(values, values.shape[2] - 1, 2)

    def face_weights(k, planes, near_x, near_y):
        k0, k1, k2 = k.at[0], k.at[1], k.at[2]
        m1, m2 = k1[planes], k2[planes]
        groups = (
            (k0[planes], (below_of(k0, planes, near_x[0]), above_of(k0, planes, near_x[1]))),
            (m1, y_shift(m1, near_y[0](planes), near_y[1](planes))),
            (m2, z_shift(m2)),
        )
        found = []
        total = k[3, planes]
        for middle, pair in groups:
            for other in pair:
                found.append(0.5 * (middle + other))
                total = total + found[-1]
        return found, total

    for j in range(4):
        for d in range(2):
            factor = 0.25 if j == d else 1.0
            if d == 0:
                for i in range(nx // 2):
                    cells[0][j, i] = (0.5 * factor) * (fields[j, 2 * i] + fields[j, 2 * i + 1])
            else:
                for planes in chunks(nx):
                    put_tiles(planes, fields[j, planes])
                for planes in chunks(nx):
                    cells[1][j, planes] = y_mean(planes) * factor
    finish(edges)
    near_rows = [kxr[0, 1], kxr[1, 0]] + [kyr[0, 1].reshape((nx, wide)), kyr[1, 0].reshape((nx, wide))]
    flat = jnp.concatenate([fields[j].reshape((rows, wide)) for j in range(4)] + near_rows, 0)
    flat = spread(flat, z_mean)
    for j in range(4):
        part = flat[rows * j:rows * (j + 1)] * (0.25 if j == 2 else 1.0)
        cells[2][j] = part.reshape(shapes[2])
    edge = flat[4 * rows:]
    edge_x = [edge[0:ny][None], edge[ny:2 * ny][None]]
    edge_y = [edge[2 * ny + nx * side:2 * ny + nx * (side + 1)].reshape((nx, 1, half + LANES)) for side in range(2)]
    put_tiles(slice(0, 2), jnp.stack([kxr[0, 1], kxr[1, 0]]))
    pair = y_mean(slice(0, 2))

    near_xs = (
        [0.125 * (kxr[side, 0:1] + kxr[side, 1:2]) for side in range(2)],
        [pair[0:1], pair[1:2]],
        edge_x,
    )

    def y_face(d, side):
        nearest = kyr.at[side, 1 - side]
        if d == 0:
            return lambda planes: jnp.concatenate(
                [0.5 * (nearest[2 * i:2 * i + 1] + nearest[2 * i + 1:2 * i + 2])
                 for i in range(planes.start, planes.stop)], 0)
        if d == 1:
            return lambda planes: 0.125 * (kyr[side, 0, planes] + kyr[side, 1, planes])
        if d == 2:
            return lambda planes: edge_y[side][planes]
        return lambda planes: nearest[planes]

    for d in range(3):
        for planes in chunks(shapes[d][0]):
            w, total_coarse = face_weights(
                cells[d], planes, near_xs[d], (y_face(d, 0), y_face(d, 1)))
            inside = cells[d][3, planes] > 0.0
            scale = jnp.where(inside, relaxation / jnp.where(inside, total_coarse, 1.0), 0.0)
            ms[d][6, planes] = scale
            for j in range(6):
                ms[d][j, planes] = w[j] * scale

    def sweep(g, slot, new_slot, keep=(0, 1, 2, 3)):
        e, yr, ys, m, f = es[g], yrs[g], yss[g], ms[g], fs[g]
        x, y, z = shapes[g]
        order = list(range(0, x, CHUNK))
        order = order[:1] + order[-1:] + order[1:-1]
        for x0 in order:
            planes = slice(x0, x0 + CHUNK)
            middle = e[slot, x0 + 1:x0 + 1 + CHUNK]
            y_low, y_high = y_shift(middle, yr[slot, 0, planes], yr[slot, 1, planes])
            z_low, z_high = z_shift(middle)
            new = (1.0 - relaxation) * middle + f[planes]
            new = new + m[0, planes] * e[slot, x0:x0 + CHUNK]
            new = new + m[1, planes] * e[slot, x0 + 2:x0 + 2 + CHUNK]
            new = new + m[2, planes] * y_low
            new = new + m[3, planes] * y_high
            new = new + m[4, planes] * z_low
            new = new + m[5, planes] * z_high
            e[new_slot, x0 + 1:x0 + 1 + CHUNK] = new
            ys[new_slot, 0, planes] = new[:, 0:1]
            ys[new_slot, 1, planes] = new[:, y - 1:y]
            if x0 == order[1] and 0 in keep:
                start(faces(g, new_slot, (0, 1)))
        if 2 in keep:
            start(faces(g, new_slot, (2, 3)))

    for cycle in range(CYCLES):
        slot = cycle % 2
        finish(faces(3, slot))
        u = es[3]
        for planes in chunks(nx):
            x0, x1 = planes.start, planes.stop
            middle = u[slot, x0 + 1:x1 + 1]
            y_low, y_high = y_shift(middle, yrs[3][slot, 0, planes], yrs[3][slot, 1, planes])
            z_low, z_high = z_shift(middle)
            w, total_fine = face_weights(
                fields, planes, (kxr[0, 1:2], kxr[1, 0:1]), (y_face(3, 0), y_face(3, 1)))
            residual = fields[4, planes] - total_fine * middle
            around = (u[slot, x0:x1], u[slot, x0 + 2:x1 + 2], y_low, y_high, z_low, z_high)
            for j in range(6):
                residual = residual + w[j] * around[j]
            put_tiles(planes, residual)
        for g in range(3):
            x, y, z = shapes[g]
            if g == 2:
                flat = get_tiles(slice(0, nx)).reshape((rows, wide))
                whole = spread(flat, z_mean).reshape(shapes[2])
            for planes in chunks(x):
                if g == 0:
                    pairs = [get_tiles(slice(2 * i, 2 * i + 2)) for i in range(planes.start, planes.stop)]
                    first = jnp.concatenate([0.5 * (p[0:1] + p[1:2]) for p in pairs], 0)
                elif g == 1:
                    first = y_mean(planes)
                else:
                    first = whole[planes]
                first = ms[g][6, planes] * first
                fs[g][planes] = first
                es[g][1, planes.start + 1:planes.stop + 1] = first
                yss[g][1, 0, planes] = first[:, 0:1]
                yss[g][1, 1, planes] = first[:, y - 1:y]
            start(faces(g, 1))

        @pl.loop(1, SWEEPS - 1)
        def _(repeat):
            old = lax.rem(repeat, 2)
            for g in range(3):
                finish(faces(g, old))
                sweep(g, old, 1 - old)

        last = SWEEPS % 2
        needed = ((0, 1), (2, 3), ())
        for g in range(3):
            finish(faces(g, 1 - last))
            sweep(g, 1 - last, last, needed[g])
        e = es[2][last, 1:nx + 1].reshape((rows, half + LANES))
        from_z = spread(e, z_spread).reshape((nx, ny, nz))
        finish(faces(1, last, needed[1]))
        for planes in chunks(nx):
            e = es[1][last, planes.start + 1:planes.stop + 1, :, :nz]
            y_low, y_high = y_shift(
                e, yrs[1][last, 0, planes, :, :nz], yrs[1][last, 1, planes, :, :nz])
            even = 0.75 * e + 0.25 * y_low
            odd = 0.75 * e + 0.25 * y_high
            for t in range(nz // LANES):
                tiles[t, planes, even_rows] = even[:, :, LANES * t:LANES * (t + 1)]
                tiles[t, planes, odd_rows] = odd[:, :, LANES * t:LANES * (t + 1)]
        finish(faces(0, last, needed[0]))
        for i in range(nx // 2):
            planes = slice(2 * i, 2 * i + 2)
            e = es[0][last, i:i + 3, :, :nz]
            even = 0.75 * e[1:2] + 0.25 * e[0:1]
            odd = 0.75 * e[1:2] + 0.25 * e[2:3]
            update = (jnp.concatenate([even, odd], 0) + get_tiles(planes, nz // LANES)) + from_z[planes]
            final = es[3][slot, 2 * i + 1:2 * i + 3, :, :nz] + blending * update
            if cycle == CYCLES - 1:
                out_ref[planes] = final
            else:
                es[3][1 - slot, 2 * i + 1:2 * i + 3, :, :nz] = final
        if cycle == CYCLES - 1:
            continue
        result = es[3].at[1 - slot, 1:nx + 1]
        per = LANES // STEP
        plane_lane = iota((ny, LANES), 1)
        groups = us.shape[1]
        for q in range(groups):
            low = jnp.zeros((ny, LANES), jnp.float32)
            high = low
            for p in range(min(per, nx - q * per)):
                here = (plane_lane >= STEP * p) & (plane_lane < STEP * p + REACH)
                first = result[q * per + p, :, :LANES]
                low = jnp.where(here, pltpu.roll(first, STEP * p, 1) if p else first, low)
                high = jnp.where(
                    here, pltpu.roll(result[q * per + p, :, nz - LANES:nz], (STEP * p + REACH) % LANES, 1), high)
            us[0, q] = low
            us[1, q] = high
        again = [
            (4, copy(us.at[0], ur.at[1], zsend.at[2], zrecv.at[2], 4)),
            (5, copy(us.at[1], ur.at[0], zsend.at[3], zrecv.at[3], 5)),
        ]
        start(again)
        finish(again)
        for i in range(nx):
            q, p = i // per, i % per
            up = pltpu.roll(ur[1, q], (LANES - STEP * p) % LANES, 1) if p else ur[1, q]
            down = pltpu.roll(ur[0, q], (2 * LANES - REACH - STEP * p) % LANES, 1)
            es[3][1 - slot, i + 1, :, nz:] = jnp.where(
                plane_lane < REACH, up, jnp.where(plane_lane >= LANES - REACH, down, 0.0))
        send_guess(1 - slot)


def body(names, right_side, coefficients, first_guess):
    nx, ny, nz = right_side.shape
    wide = nz + LANES
    shapes = ((nx // 2, ny, wide), (nx, ny // 2, wide), (nx, ny, nz // 2 + LANES), (nx, ny, wide))
    f32 = jnp.float32
    vmem = lambda *shape: pltpu.VMEM(shape, f32)
    dma = pltpu.SemaphoreType.DMA
    groups = -(-nx // (LANES // STEP))
    scratch = [
        vmem(5, nx, ny, wide),
        tuple(vmem(4, x, y, z) for x, y, z in shapes[:3]),
        vmem(wide // LANES, nx, ny, LANES),
        tuple(vmem(2, x + 2, y, z) for x, y, z in shapes),
        tuple(vmem(2, 2, x, 1, z) for x, y, z in shapes),
        tuple(vmem(2, 2, x, 1, z) for x, y, z in shapes),
        tuple(vmem(7, x, y, z) for x, y, z in shapes[:3]),
        tuple(vmem(x, y, z) for x, y, z in shapes[:3]),
        vmem(2, 2, ny, wide),
        vmem(2, 2, nx, 1, wide),
        vmem(2, 2, nx, 1, wide),
        vmem(2, nx, ny, LANES),
        vmem(2, nx, ny, LANES),
        vmem(2, groups, ny, LANES),
        vmem(2, groups, ny, LANES),
        dma((4, 4, 2)), dma((4, 4, 2)), dma((4,)), dma((4,)), dma((4,)), dma((4,)),
    ]
    spec = pl.BlockSpec(memory_space=pltpu.VMEM)
    return pl.pallas_call(
        functools.partial(kernel, (nx, ny, nz), names),
        out_shape=jax.ShapeDtypeStruct(right_side.shape, f32),
        in_specs=[spec] * 3,
        out_specs=spec,
        scratch_shapes=scratch,
        compiler_params=pltpu.CompilerParams(
            collective_id=0, has_side_effects=True, vmem_limit_bytes=60 * 1024 * 1024),
    )(right_side, coefficients, first_guess)


def solution(mesh):
    names = tuple(mesh.axis_names)
    in_specs = (P(*names), P(None, *names), P(*names))
    return jax.shard_map(
        functools.partial(body, names), mesh=mesh, in_specs=in_specs, out_specs=P(*names),
        check_vma=False)
```

```python
import functools

import jax
import jax.numpy as jnp
from jax import lax
from jax.experimental import pallas as pl
from jax.experimental.pallas import tpu as pltpu
from jax.sharding import PartitionSpec as P

CYCLES = 2
SWEEPS = 8
REACH = 2 * (SWEEPS + 1)
STEP = 20
LANES = 128
CHUNK = 1

relaxation = 0.8
blending = 0.4
MESH = pl.DeviceIdType.MESH


def iota(shape, dim):
    return lax.broadcasted_iota(jnp.int32, shape, dim)


def spread(a, b):
    total = None
    for _ in range(3):
        part = a.astype(jnp.bfloat16)
        a = a - part.astype(jnp.float32)
        term = jnp.dot(part, b, preferred_element_type=jnp.float32)
        total = term if total is None else total + term
    return total


def kernel(sizes, names, b_ref, k_ref, g_ref, out_ref, *scratch):
    (fields, cells, tiles, es, yss, yrs, ms, fs, kxr, kys, kyr, zs, zr, us, ur,
     send, recv, ksend, krecv, zsend, zrecv) = scratch
    nx, ny, nz = sizes
    wide = nz + LANES
    shapes = ((nx // 2, ny, wide), (nx, ny // 2, wide), (nx, ny, nz // 2 + LANES), (nx, ny, wide))
    place = [lax.axis_index(n) for n in names]
    counts = [lax.axis_size(n) for n in names]
    has_low = [p > 0 for p in place]
    has_high = [p < c - 1 for p, c in zip(place, counts)]
    ways = []
    for axis in range(3):
        ways.append((axis, -1, has_low[axis], has_high[axis]))
        ways.append((axis, 1, has_high[axis], has_low[axis]))

    def target(way):
        axis, step = ways[way][:2]
        return {names[axis]: place[axis] + step}

    def copy(src, dst, ssem, rsem, way):
        return pltpu.make_async_remote_copy(
            src_ref=src, dst_ref=dst, send_sem=ssem, recv_sem=rsem,
            device_id=target(way), device_id_type=MESH,
        )

    def start(copies):
        for way, c in copies:
            @pl.when(ways[way][2])
            def _():
                c.start()

    def finish(copies):
        for way, c in copies:
            @pl.when(ways[way][3])
            def _():
                c.wait_recv()
        for way, c in copies:
            @pl.when(ways[way][2])
            def _():
                c.wait_send()

    def faces(g, slot, keep=(0, 1, 2, 3)):
        x = shapes[g][0]
        e, ys, yr = es[g], yss[g], yrs[g]
        ends = (
            (e.at[slot, 1], e.at[slot, x + 1]),
            (e.at[slot, x], e.at[slot, 0]),
            (ys.at[slot, 0], yr.at[slot, 1]),
            (ys.at[slot, 1], yr.at[slot, 0]),
        )
        return [
            (way, copy(*ends[way], send.at[g, way, slot], recv.at[g, way, slot], way)) for way in keep
        ]

    for g in range(4):
        x = shapes[g][0]
        for slot in range(2):
            zero = jnp.zeros(shapes[g][1:], jnp.float32)
            es[g][slot, 0] = zero
            es[g][slot, x + 1] = zero
        yrs[g][...] = jnp.zeros(yrs[g].shape, jnp.float32)
    kxr[...] = jnp.zeros(kxr.shape, jnp.float32)
    kyr[...] = jnp.zeros(kyr.shape, jnp.float32)
    zr[...] = jnp.zeros(zr.shape, jnp.float32)
    ur[...] = jnp.zeros(ur.shape, jnp.float32)

    barrier = pltpu.get_barrier_semaphore()
    for way in range(6):
        @pl.when(ways[way][2])
        def _():
            pl.semaphore_signal(barrier, inc=1, device_id=target(way), device_id_type=MESH)
    peers = sum(jnp.where(has, 1, 0) for has in has_low + has_high)
    pl.semaphore_wait(barrier, peers)

    lane = iota((nx, ny, LANES), 2)
    low = jnp.zeros((nx, ny, LANES), jnp.float32)
    high = low
    for j in range(6):
        if j < 4:
            first, last = k_ref[j, :, :, :LANES], k_ref[j, :, :, nz - LANES:]
        elif j == 4:
            first, last = g_ref[:, :, :LANES], g_ref[:, :, nz - LANES:]
        else:
            first, last = b_ref[:, :, :LANES], b_ref[:, :, nz - LANES:]
        here = (lane >= STEP * j) & (lane < STEP * j + REACH)
        low = jnp.where(here, pltpu.roll(first, STEP * j, 2) if j else first, low)
        high = jnp.where(here, pltpu.roll(last, (STEP * j + REACH) % LANES, 2), high)
    zs[0] = low
    zs[1] = high
    deep = [
        (4, copy(zs.at[0], zr.at[1], zsend.at[0], zrecv.at[0], 4)),
        (5, copy(zs.at[1], zr.at[0], zsend.at[1], zrecv.at[1], 5)),
    ]
    start(deep)
    for j in range(4):
        fields[j, :, :, :nz] = k_ref[j]
    fields[4, :, :, :nz] = b_ref[...]
    es[3][0, 1:nx + 1, :, :nz] = g_ref[...]
    finish(deep)
    above, below = zr[1], zr[0]

    def beside(j):
        up = pltpu.roll(above, (LANES - STEP * j) % LANES, 2) if j else above
        down = pltpu.roll(below, (2 * LANES - REACH - STEP * j) % LANES, 2)
        return jnp.where(lane < REACH, up, jnp.where(lane >= LANES - REACH, down, 0.0))

    for j in range(4):
        fields[j, :, :, nz:] = beside(j)
    es[3][0, 1:nx + 1, :, nz:] = beside(4)
    fields[4, :, :, nz:] = beside(5)

    def send_guess(slot):
        u = es[3][slot, 1:nx + 1]
        yss[3][slot, 0] = u[:, 0:1, :]
        yss[3][slot, 1] = u[:, ny - 1:ny, :]
        start(faces(3, slot))

    ky = fields[1]
    for row in range(2):
        kys[0, row] = ky[:, row:row + 1, :]
        kys[1, row] = ky[:, ny - 2 + row:ny - 1 + row, :]
    edges = [
        (0, copy(fields.at[0, pl.ds(0, 2)], kxr.at[1], ksend.at[0], krecv.at[0], 0)),
        (1, copy(fields.at[0, pl.ds(nx - 2, 2)], kxr.at[0], ksend.at[1], krecv.at[1], 1)),
        (2, copy(kys.at[0], kyr.at[1], ksend.at[2], krecv.at[2], 2)),
        (3, copy(kys.at[1], kyr.at[0], ksend.at[3], krecv.at[3], 3)),
    ]
    start(edges)
    send_guess(0)

    half = nz // 2
    r, c = iota((wide, half + LANES), 0), iota((wide, half + LANES), 1)
    home = jnp.where(
        r < nz, r // 2,
        jnp.where(r < nz + LANES // 2, half + (r - nz) // 2, half + LANES // 2 + (r - nz) // 2),
    )
    z_mean = jnp.where(home == c, 0.5, 0.0).astype(jnp.bfloat16)
    rows = nx * ny
    r, c = iota((half + LANES, nz), 0), iota((half + LANES, nz), 1)
    main = c // 2
    total = half + LANES
    side = jnp.where(c % 2 == 1, main + 1, jnp.where(main == 0, total - 1, main - 1))
    z_spread = (jnp.where(r == main, 0.75, 0.0) + jnp.where(r == side, 0.25, 0.0)).astype(jnp.bfloat16)

    count = wide // LANES
    even_rows, odd_rows = pl.ds(0, ny // 2, stride=2), pl.ds(1, ny // 2, stride=2)

    def put_tiles(planes, values):
        for t in range(values.shape[2] // LANES):
            tiles[t, planes] = values[:, :, LANES * t:LANES * (t + 1)]

    def get_tiles(planes, tiles_of=count):
        return jnp.concatenate([tiles[t, planes] for t in range(tiles_of)], 2)

    def y_mean(planes):
        return jnp.concatenate(
            [0.5 * (tiles[t, planes, even_rows] + tiles[t, planes, odd_rows]) for t in range(count)], 2)

    def chunks(x, step=CHUNK):
        return [slice(x0, x0 + step) for x0 in range(0, x, step)]

    def below_of(ref, planes, halo):
        if planes.start > 0:
            return ref[planes.start - 1:planes.stop - 1]
        return halo if planes.stop == 1 else jnp.concatenate([halo, ref[0:planes.stop - 1]], 0)

    def above_of(ref, planes, halo):
        if planes.stop < ref.shape[0]:
            return ref[planes.start + 1:planes.stop + 1]
        if planes.stop == planes.start + 1:
            return halo
        return jnp.concatenate([ref[planes.start + 1:planes.stop], halo], 0)

    def y_shift(values, halo_low, halo_high):
        y = values.shape[1]
        row = iota(values.shape, 1)
        lower = jnp.where(row == 0, halo_low, pltpu.roll(values, 1, 1))
        upper = jnp.where(row == y - 1, halo_high, pltpu.roll(values, y - 1, 1))
        return lower, upper

    def z_shift(values):
        return pltpu.roll(values, 1, 2), pltpu.roll(values, values.shape[2] - 1, 2)

    def face_weights(k, planes, near_x, near_y):
        k0, k1, k2 = k.at[0], k.at[1], k.at[2]
        m1, m2 = k1[planes], k2[planes]
        groups = (
            (k0[planes], (below_of(k0, planes, near_x[0]), above_of(k0, planes, near_x[1]))),
            (m1, y_shift(m1, near_y[0](planes), near_y[1](planes))),
            (m2, z_shift(m2)),
        )
        found = []
        total = k[3, planes]
        for middle, pair in groups:
            for other in pair:
                found.append(0.5 * (middle + other))
                total = total + found[-1]
        return found, total

    for j in range(4):
        for d in range(2):
            factor = 0.25 if j == d else 1.0
            if d == 0:
                for i in range(nx // 2):
                    cells[0][j, i] = (0.5 * factor) * (fields[j, 2 * i] + fields[j, 2 * i + 1])
            else:
                for planes in chunks(nx):
                    put_tiles(planes, fields[j, planes])
                for planes in chunks(nx):
                    cells[1][j, planes] = y_mean(planes) * factor
    for j in range(4):
        factor = 0.25 if j == 2 else 1.0
        for planes in chunks(nx, nx // 2):
            flat = fields[j, planes].reshape((rows // 2, wide))
            cells[2][j, planes] = (spread(flat, z_mean) * factor).reshape((nx // 2,) + shapes[2][1:])
    finish(edges)
    near_rows = [kxr[0, 1], kxr[1, 0]] + [kyr[0, 1].reshape((nx, wide)), kyr[1, 0].reshape((nx, wide))]
    edge = spread(jnp.concatenate(near_rows, 0), z_mean)
    edge_x = [edge[0:ny][None], edge[ny:2 * ny][None]]
    edge_y = [edge[2 * ny + nx * side:2 * ny + nx * (side + 1)].reshape((nx, 1, half + LANES)) for side in range(2)]
    put_tiles(slice(0, 2), jnp.stack([kxr[0, 1], kxr[1, 0]]))
    pair = y_mean(slice(0, 2))

    near_xs = (
        [0.125 * (kxr[side, 0:1] + kxr[side, 1:2]) for side in range(2)],
        [pair[0:1], pair[1:2]],
        edge_x,
    )

    def y_face(d, side):
        nearest = kyr.at[side, 1 - side]
        if d == 0:
            return lambda planes: jnp.concatenate(
                [0.5 * (nearest[2 * i:2 * i + 1] + nearest[2 * i + 1:2 * i + 2])
                 for i in range(planes.start, planes.stop)], 0)
        if d == 1:
            return lambda planes: 0.125 * (kyr[side, 0, planes] + kyr[side, 1, planes])
        if d == 2:
            return lambda planes: edge_y[side][planes]
        return lambda planes: nearest[planes]

    for d in range(3):
        for planes in chunks(shapes[d][0]):
            w, total_coarse = face_weights(
                cells[d], planes, near_xs[d], (y_face(d, 0), y_face(d, 1)))
            inside = cells[d][3, planes] > 0.0
            scale = jnp.where(inside, relaxation / jnp.where(inside, total_coarse, 1.0), 0.0)
            ms[d][6, planes] = scale
            for j in range(6):
                ms[d][j, planes] = w[j] * scale

    def sweep(g, slot, new_slot, keep=(0, 1, 2, 3)):
        e, yr, ys, m, f = es[g], yrs[g], yss[g], ms[g], fs[g]
        x, y, z = shapes[g]
        order = list(range(0, x, CHUNK))
        order = order[:1] + order[-1:] + order[1:-1]
        for x0 in order:
            planes = slice(x0, x0 + CHUNK)
            middle = e[slot, x0 + 1:x0 + 1 + CHUNK]
            y_low, y_high = y_shift(middle, yr[slot, 0, planes], yr[slot, 1, planes])
            z_low, z_high = z_shift(middle)
            new = (1.0 - relaxation) * middle + f[planes]
            new = new + m[0, planes] * e[slot, x0:x0 + CHUNK]
            new = new + m[1, planes] * e[slot, x0 + 2:x0 + 2 + CHUNK]
            new = new + m[2, planes] * y_low
            new = new + m[3, planes] * y_high
            new = new + m[4, planes] * z_low
            new = new + m[5, planes] * z_high
            e[new_slot, x0 + 1:x0 + 1 + CHUNK] = new
            ys[new_slot, 0, planes] = new[:, 0:1]
            ys[new_slot, 1, planes] = new[:, y - 1:y]
            if x0 == order[1] and 0 in keep:
                start(faces(g, new_slot, (0, 1)))
        if 2 in keep:
            start(faces(g, new_slot, (2, 3)))

    for cycle in range(CYCLES):
        slot = cycle % 2
        finish(faces(3, slot))
        u = es[3]
        for planes in chunks(nx):
            x0, x1 = planes.start, planes.stop
            middle = u[slot, x0 + 1:x1 + 1]
            y_low, y_high = y_shift(middle, yrs[3][slot, 0, planes], yrs[3][slot, 1, planes])
            z_low, z_high = z_shift(middle)
            w, total_fine = face_weights(
                fields, planes, (kxr[0, 1:2], kxr[1, 0:1]), (y_face(3, 0), y_face(3, 1)))
            residual = fields[4, planes] - total_fine * middle
            around = (u[slot, x0:x1], u[slot, x0 + 2:x1 + 2], y_low, y_high, z_low, z_high)
            for j in range(6):
                residual = residual + w[j] * around[j]
            put_tiles(planes, residual)
        for g in range(3):
            x, y, z = shapes[g]
            if g == 2:
                flat = get_tiles(slice(0, nx)).reshape((rows, wide))
                whole = spread(flat, z_mean).reshape(shapes[2])
            for planes in chunks(x):
                if g == 0:
                    pairs = [get_tiles(slice(2 * i, 2 * i + 2)) for i in range(planes.start, planes.stop)]
                    first = jnp.concatenate([0.5 * (p[0:1] + p[1:2]) for p in pairs], 0)
                elif g == 1:
                    first = y_mean(planes)
                else:
                    first = whole[planes]
                first = ms[g][6, planes] * first
                fs[g][planes] = first
                es[g][1, planes.start + 1:planes.stop + 1] = first
                yss[g][1, 0, planes] = first[:, 0:1]
                yss[g][1, 1, planes] = first[:, y - 1:y]
            start(faces(g, 1))

        @pl.loop(1, SWEEPS - 1)
        def _(repeat):
            old = lax.rem(repeat, 2)
            for g in range(3):
                finish(faces(g, old))
                sweep(g, old, 1 - old)

        last = SWEEPS % 2
        needed = ((0, 1), (2, 3), ())
        for g in range(3):
            finish(faces(g, 1 - last))
            sweep(g, 1 - last, last, needed[g])
        e = es[2][last, 1:nx + 1].reshape((rows, half + LANES))
        from_z = spread(e, z_spread).reshape((nx, ny, nz))
        finish(faces(1, last, needed[1]))
        for planes in chunks(nx):
            e = es[1][last, planes.start + 1:planes.stop + 1, :, :nz]
            y_low, y_high = y_shift(
                e, yrs[1][last, 0, planes, :, :nz], yrs[1][last, 1, planes, :, :nz])
            even = 0.75 * e + 0.25 * y_low
            odd = 0.75 * e + 0.25 * y_high
            for t in range(nz // LANES):
                tiles[t, planes, even_rows] = even[:, :, LANES * t:LANES * (t + 1)]
                tiles[t, planes, odd_rows] = odd[:, :, LANES * t:LANES * (t + 1)]
        finish(faces(0, last, needed[0]))
        for i in range(nx // 2):
            planes = slice(2 * i, 2 * i + 2)
            e = es[0][last, i:i + 3, :, :nz]
            even = 0.75 * e[1:2] + 0.25 * e[0:1]
            odd = 0.75 * e[1:2] + 0.25 * e[2:3]
            update = (jnp.concatenate([even, odd], 0) + get_tiles(planes, nz // LANES)) + from_z[planes]
            final = es[3][slot, 2 * i + 1:2 * i + 3, :, :nz] + blending * update
            if cycle == CYCLES - 1:
                out_ref[planes] = final
            else:
                es[3][1 - slot, 2 * i + 1:2 * i + 3, :, :nz] = final
        if cycle == CYCLES - 1:
            continue
        result = es[3].at[1 - slot, 1:nx + 1]
        per = LANES // STEP
        plane_lane = iota((ny, LANES), 1)
        groups = us.shape[1]
        for q in range(groups):
            low = jnp.zeros((ny, LANES), jnp.float32)
            high = low
            for p in range(min(per, nx - q * per)):
                here = (plane_lane >= STEP * p) & (plane_lane < STEP * p + REACH)
                first = result[q * per + p, :, :LANES]
                low = jnp.where(here, pltpu.roll(first, STEP * p, 1) if p else first, low)
                high = jnp.where(
                    here, pltpu.roll(result[q * per + p, :, nz - LANES:nz], (STEP * p + REACH) % LANES, 1), high)
            us[0, q] = low
            us[1, q] = high
        again = [
            (4, copy(us.at[0], ur.at[1], zsend.at[2], zrecv.at[2], 4)),
            (5, copy(us.at[1], ur.at[0], zsend.at[3], zrecv.at[3], 5)),
        ]
        start(again)
        finish(again)
        for i in range(nx):
            q, p = i // per, i % per
            up = pltpu.roll(ur[1, q], (LANES - STEP * p) % LANES, 1) if p else ur[1, q]
            down = pltpu.roll(ur[0, q], (2 * LANES - REACH - STEP * p) % LANES, 1)
            es[3][1 - slot, i + 1, :, nz:] = jnp.where(
                plane_lane < REACH, up, jnp.where(plane_lane >= LANES - REACH, down, 0.0))
        send_guess(1 - slot)


def body(names, right_side, coefficients, first_guess):
    nx, ny, nz = right_side.shape
    wide = nz + LANES
    shapes = ((nx // 2, ny, wide), (nx, ny // 2, wide), (nx, ny, nz // 2 + LANES), (nx, ny, wide))
    f32 = jnp.float32
    vmem = lambda *shape: pltpu.VMEM(shape, f32)
    dma = pltpu.SemaphoreType.DMA
    groups = -(-nx // (LANES // STEP))
    scratch = [
        vmem(5, nx, ny, wide),
        tuple(vmem(4, x, y, z) for x, y, z in shapes[:3]),
        vmem(wide // LANES, nx, ny, LANES),
        tuple(vmem(2, x + 2, y, z) for x, y, z in shapes),
        tuple(vmem(2, 2, x, 1, z) for x, y, z in shapes),
        tuple(vmem(2, 2, x, 1, z) for x, y, z in shapes),
        tuple(vmem(7, x, y, z) for x, y, z in shapes[:3]),
        tuple(vmem(x, y, z) for x, y, z in shapes[:3]),
        vmem(2, 2, ny, wide),
        vmem(2, 2, nx, 1, wide),
        vmem(2, 2, nx, 1, wide),
        vmem(2, nx, ny, LANES),
        vmem(2, nx, ny, LANES),
        vmem(2, groups, ny, LANES),
        vmem(2, groups, ny, LANES),
        dma((4, 4, 2)), dma((4, 4, 2)), dma((4,)), dma((4,)), dma((4,)), dma((4,)),
    ]
    spec = pl.BlockSpec(memory_space=pltpu.VMEM)
    return pl.pallas_call(
        functools.partial(kernel, (nx, ny, nz), names),
        out_shape=jax.ShapeDtypeStruct(right_side.shape, f32),
        in_specs=[spec] * 3,
        out_specs=spec,
        scratch_shapes=scratch,
        compiler_params=pltpu.CompilerParams(
            collective_id=0, has_side_effects=True, vmem_limit_bytes=60 * 1024 * 1024),
    )(right_side, coefficients, first_guess)


def solution(mesh):
    names = tuple(mesh.axis_names)
    in_specs = (P(*names), P(None, *names), P(*names))
    return jax.shard_map(
        functools.partial(body, names), mesh=mesh, in_specs=in_specs, out_specs=P(*names),
        check_vma=False)
```
